512 devices in a mesh: seq: 128 (over y, x_lo, z), tp: 4 (over x_hi, core).
Axes of the slice: x: 4 (x_hi: 2, x_lo: 2; x = x_hi * 2 + x_lo), y: 4, z: 16, core: 2. Of those that a mesh axis runs over, the one named last changes fastest.
Arguments:
- query: bfloat16 [24576, 2560], P('seq', 'tp'), may hold values from -9 to 9
- keys: bfloat16 [28672, 2560], P('seq', 'tp'), may hold values from -9 to 9
- values: bfloat16 [28672, 2560], P('seq', 'tp'), may hold values from -6 to 6
- q_gain: float32 [64], replicated, may hold values from 1.8 to 7
- k_gain: float32 [2, 64], replicated, may hold values from 1.8 to 7
- residual: bfloat16 [24576, 2432], P('seq', 'tp'), may hold values from -6 to 6
- gate: bfloat16 [8, 2432], P(None, 'tp'), may hold values from -5 to 5
- out_weight: bfloat16 [2560, 2432], P('tp'), may hold values from -0.125 to 0.125
- image_count: int32 [8], replicated, may hold values from 1536 to 3072, as said below
Outputs:
- updated: bfloat16 [24576, 2432], P('seq', 'tp')
The draws below stay inside these ranges and needn't reach their ends.
Inputs may be any that keep to these rules, and one draw needn't show every extreme that they name: Request g's live image tokens are its first image_count[g] image slots; in every draw some request has all 3072 live.
All inputs are finite; a program needn't handle non-finite values.
Results may differ from the reference program's by a relative error of at most 0.025.
Values may be sent and summed in bfloat16 or wider, within the bound.
A program may use at most 128 MiB of HBM per device.

```python
import jax
import jax.numpy as jnp
from jax import lax

D = 2432
HEADS = 38
HEAD_DIM = 64
IMG_DEV = 192
HEADS_DEV = 10
HEAD_SLOTS = 40
REQ_DEV = 16
REQUESTS = 8
KV_DEV = 224
IMG_REQ = 3072
IMG_TOTAL = 24576
KV_TOTAL = 28672
N_SEQ = 128
N_TP = 4


def base_keys(key):
    return jax.random.normal(jax.random.fold_in(key, 11), (KV_TOTAL, HEAD_SLOTS * HEAD_DIM), jnp.float32)


def draw_keys(key, part):
    drawn = base_keys(key)
    return drawn.astype(jnp.bfloat16)


def draw_query(key, part):
    drawn = jax.random.normal(jax.random.fold_in(key, 12), (IMG_TOTAL, HEAD_SLOTS * HEAD_DIM), jnp.float32)
    return drawn.astype(jnp.bfloat16)


def draw_q_gain(key, part):
    return jax.random.uniform(jax.random.fold_in(key, 31), (HEAD_DIM,), jnp.float32, 1.8, 2.6)


def draw_k_gain(key, part):
    return jax.random.uniform(jax.random.fold_in(key, 32), (2, HEAD_DIM), jnp.float32, 1.8, 2.6)


def draw_image_count(key, part):
    top_count = IMG_REQ
    low_count = IMG_REQ // 2
    counts = jax.random.randint(jax.random.fold_in(key, 21), (REQUESTS,), low_count, top_count + 1, dtype=jnp.int32)
    chosen = jax.random.randint(jax.random.fold_in(key, 22), (), 0, REQUESTS, dtype=jnp.int32)
    counts = jnp.where(jnp.arange(REQUESTS, dtype=jnp.int32) == chosen, top_count, counts)
    return counts.astype(jnp.int32)


def level_of(rng, dims, pieces, least, high):
    def one(axis_at, parts):
        heights = jax.random.uniform(jax.random.fold_in(jax.random.fold_in(rng, 6), axis_at), (parts,), jnp.float32, least / len(pieces), high / len(pieces))
        return jnp.repeat(jnp.exp(heights), dims[axis_at] // parts).reshape((-1,) + (1,) * (len(dims) - axis_at - 1))

    level = one(*pieces[0])
    for cut in pieces[1:]:
        level = level * one(*cut)
    return level


def centred(key, shape, deviation, reach, split=(), kind=jnp.bfloat16):
    gain = level_of(key, shape, split, -0.22, 0.18) if split else 1.0
    values = jax.random.normal(key, shape, jnp.float32) * deviation * gain
    return jnp.minimum(jnp.maximum(values, -reach), reach).astype(kind)


def setup_inputs(seed: int = 0) -> dict:
    key_of = jax.random.split(jax.random.key(seed), 10)
    return {
        "query": draw_query(jax.random.fold_in(key_of[9], 71), 0),
        "keys": draw_keys(jax.random.fold_in(key_of[9], 71), 0),
        "values": centred(key_of[2], (KV_TOTAL, HEAD_SLOTS * HEAD_DIM), 1.0, 6.0, ((0, 128), (1, 4))),
        "q_gain": draw_q_gain(jax.random.fold_in(key_of[9], 71), 0),
        "k_gain": draw_k_gain(jax.random.fold_in(key_of[9], 71), 0),
        "residual": centred(key_of[5], (IMG_TOTAL, D), 1.0, 6.0, ((0, 128), (1, 4))),
        "gate": centred(key_of[6], (REQUESTS, D), 1.0, 5.0, ((1, 4),)),
        "out_weight": centred(key_of[7], (HEAD_SLOTS * HEAD_DIM, D), (HEADS * HEAD_DIM) ** -0.5, 0.125, ((0, 4),)),
        "image_count": draw_image_count(jax.random.fold_in(key_of[9], 71), 0),
    }


epsilon = 1e-06

def rms_scale(values_in, gain_rows):
    inverse = lax.rsqrt(lax.optimization_barrier(jnp.mean(values_in * values_in, axis=-1, keepdims=True)) + epsilon)
    return values_in * inverse * gain_rows

def reference(query, keys, values, q_gain, k_gain, residual, gate, out_weight, image_count):
    query_float = query.astype(jnp.float32).reshape(IMG_TOTAL, HEAD_SLOTS, HEAD_DIM)
    query_normed = rms_scale(query_float, q_gain.astype(jnp.float32)).astype(jnp.bfloat16)
    key_float = keys.astype(jnp.float32).reshape(N_SEQ, KV_DEV, HEAD_SLOTS, HEAD_DIM)
    text_rows = jnp.arange(KV_DEV, dtype=jnp.int32) >= IMG_DEV
    gains = k_gain.astype(jnp.float32)
    key_gain_rows = jnp.where(text_rows[:, None], gains[1][None, :], gains[0][None, :])
    key_normed = rms_scale(key_float, key_gain_rows[None, :, None, :]).astype(jnp.bfloat16)
    query_req = query_normed.reshape(REQUESTS, IMG_REQ, HEAD_SLOTS, HEAD_DIM)
    key_req = key_normed.reshape(REQUESTS, REQ_DEV * KV_DEV, HEAD_SLOTS, HEAD_DIM)
    value_req = values.reshape(REQUESTS, REQ_DEV * KV_DEV, HEAD_SLOTS, HEAD_DIM)
    key_index = jnp.arange(REQ_DEV * KV_DEV, dtype=jnp.int32)
    block_rank = key_index // KV_DEV
    within = key_index % KV_DEV
    slots = jnp.arange(HEAD_SLOTS, dtype=jnp.int32)
    head_valid = (slots % HEADS_DEV < (HEADS + N_TP - 1 - slots // HEADS_DEV) // N_TP).astype(jnp.float32)
    score_scale = HEAD_DIM ** (-0.5)

    def one_request(inputs):
        query_rows, key_rows, value_rows, live_count = inputs
        live = (within >= IMG_DEV) | (block_rank * IMG_DEV + within < live_count)

        def one_head(head_index):
            query_head = query_rows[:, head_index]
            key_head = key_rows[:, head_index]
            value_head = value_rows[:, head_index]
            scores = lax.dot_general(query_head, key_head, (((1,), (1,)), ((), ())), preferred_element_type=jnp.float32) * score_scale
            scores = jnp.where(live[None, :], scores, -1e+30)
            maxima = lax.optimization_barrier(jnp.max(scores, axis=1, keepdims=True))
            expd = jnp.exp(scores - maxima)
            weights = (expd / lax.optimization_barrier(jnp.sum(expd, axis=1, keepdims=True))).astype(jnp.bfloat16)
            return jnp.dot(weights, value_head, preferred_element_type=jnp.float32)
        return lax.map(one_head, jnp.arange(HEAD_SLOTS, dtype=jnp.int32))
    attended = lax.map(one_request, (query_req, key_req, value_req, image_count))
    attended = attended * head_valid[None, :, None, None]
    attended = jnp.transpose(attended, (0, 2, 1, 3)).reshape(IMG_TOTAL, HEAD_SLOTS * HEAD_DIM).astype(jnp.bfloat16)
    projected = jnp.dot(attended, out_weight, preferred_element_type=jnp.float32)
    gate_rows = jnp.repeat(gate.astype(jnp.float32), IMG_REQ, axis=0)
    return (residual.astype(jnp.float32) + gate_rows * projected).astype(jnp.bfloat16)
```

```python
import jax
import jax.numpy as jnp
from jax import lax
from jax.experimental import pallas as pl
from jax.experimental.pallas import tpu as pltpu
from jax.sharding import PartitionSpec as P

HEADS = 38
HEAD_DIM = 64
RING = 16
SLOTS = 10
IMG = 192
KEYS = 224
HALF = IMG // 2
PAIR = 2 * HEAD_DIM
CHUNK = 4 * IMG
STEP = 2 * KEYS
LOG2E = 1.4426950408889634
MESH = pl.DeviceIdType.MESH
epsilon = 1e-06


def lanes(shape):
    return lax.broadcasted_iota(jnp.int32, shape, 1)


def pack(low, high):
    first = lanes(low.shape) < HEAD_DIM
    even = jnp.where(first, low, pltpu.roll(high, HEAD_DIM, 1))
    odd = jnp.where(first, pltpu.roll(low, HEAD_DIM, 1), high)
    return even.astype(jnp.bfloat16), odd.astype(jnp.bfloat16)


def normed(value, gain, ones):
    x = value.astype(jnp.float32)
    square = x * x
    high = square.astype(jnp.bfloat16)
    low = (square - high.astype(jnp.float32)).astype(jnp.bfloat16)
    total = jnp.dot(high, ones, preferred_element_type=jnp.float32)
    total += jnp.dot(low, ones, preferred_element_type=jnp.float32)
    inverse = lax.rsqrt(total * (1.0 / HEAD_DIM) + epsilon)
    return (x * inverse * gain).astype(jnp.bfloat16).astype(jnp.float32)


def prep_kernel(count_ref, q_ref, k_ref, v_ref, qg_ref, kg_ref, qp_ref, kvp_ref):
    pos = lax.axis_index("seq")
    rank = lax.rem(pos, RING)
    left = count_ref[lax.div(pos, RING)] - rank * IMG
    row = lax.broadcasted_iota(jnp.int32, (PAIR, PAIR), 0) < HEAD_DIM
    column = lanes((PAIR, PAIR)) < HEAD_DIM
    ones = jnp.where(row == column, 1.0, 0.0).astype(jnp.bfloat16)
    q_gain = jnp.concatenate([qg_ref[...], qg_ref[...]], axis=1)
    k_gain = jnp.concatenate([kg_ref[...], kg_ref[...]], axis=1)
    key_row = lax.broadcasted_iota(jnp.int32, (KEYS, PAIR), 0)
    gain_rows = jnp.where(key_row < IMG, k_gain[0:1], k_gain[1:2])
    dead = (key_row < IMG) & (key_row >= left)
    for p in range(SLOTS // 2):
        columns = slice(p * PAIR, (p + 1) * PAIR)
        q = normed(q_ref[:, columns], q_gain, ones) * HEAD_DIM ** (-0.5)
        qp_ref[2 * p], qp_ref[2 * p + 1] = pack(q[:HALF], q[HALF:])
        k = normed(k_ref[:, columns], gain_rows, ones)
        k = jnp.where(dead, k[IMG : IMG + 1], k)
        v = jnp.where(dead, 0.0, v_ref[:, columns].astype(jnp.float32))
        kvp_ref[2 * p], kvp_ref[2 * p + 1] = pack(k, v)


def near(i):
    return RING + (2 * lax.rem(i, 2) - 1) * lax.div(i + 1, 2)


def role(z, core):
    part, quarter = lax.rem(z, 4), lax.div(z, 4)
    double = lax.div(4 - part, 4)
    odd = lax.rem(part, 2)
    middle = (1 - double) * (1 - odd)
    owner = double * core + odd * lax.div(part, 2) + middle * lax.rem(quarter, 2)
    slot = double * quarter + odd * (4 + quarter) + middle * (8 + lax.div(z, 8))
    return double, owner, slot


def main_kernel(
    count_ref, qp_ref, kvp_ref, att_ref,
    kv_buf, q_buf, q_all, m_all, acc_all, o_stage, o_buf,
    kv_send, kv_recv, q_send, q_recv, o_send, o_recv, relay_send,
):
    pos = lax.axis_index("seq")
    tp = lax.axis_index("tp")
    z = lax.rem(pos, RING)
    base = pos - z
    core = lax.rem(tp, 2)
    tp_base = tp - core
    double, owner, my_slot = role(z, core)
    parity = lax.rem(z, 2)

    barrier = pltpu.get_barrier_semaphore()
    linear = z * 2 + core

    def greet(i, _):
        peer = lax.rem(linear + i, 2 * RING)
        pl.semaphore_signal(
            barrier,
            inc=1,
            device_id=(base + lax.div(peer, 2), tp_base + lax.rem(peer, 2)),
            device_id_type=MESH,
        )
        return 0

    lax.fori_loop(1, 2 * RING, greet, 0)
    pl.semaphore_wait(barrier, 2 * RING - 1)

    def target(i):
        chip = lax.rem(z + 2 * RING - near(i), RING)
        return (chip,) + role(chip, core)

    def q_copy(i):
        chip, dbl, _, slot = target(i)
        to_core = dbl * core + (1 - dbl) * parity
        place = dbl * z + (1 - dbl) * lax.div(z, 2)
        return pltpu.make_async_remote_copy(
            src_ref=qp_ref.at[slot], dst_ref=q_buf.at[place],
            send_sem=q_send.at[i], recv_sem=q_recv.at[place],
            device_id=(base + chip, tp_base + to_core), device_id_type=MESH,
        )

    q_local = double * z + (1 - double) * lax.div(z, 2)
    q_stays = (owner == core) & ((double == 1) | (parity == core))

    def q_start(k, _):
        i = RING - 1 - k

        @pl.when(target(i)[2] == core)
        def _():
            q_copy(i).start()

        return 0

    lax.fori_loop(0, RING - 1, q_start, 0)

    @pl.when(q_stays)
    def _():
        pltpu.make_async_copy(qp_ref.at[my_slot], q_buf.at[q_local], q_recv.at[q_local]).start()

    @pl.when((owner == core) & jnp.logical_not(q_stays))
    def _():
        q_copy(0).start()

    def kv_copy(i):
        chip, _, _, slot = target(i)
        return pltpu.make_async_remote_copy(
            src_ref=kvp_ref.at[slot], dst_ref=kv_buf.at[i],
            send_sem=kv_send.at[i], recv_sem=kv_recv.at[i],
            device_id=(base + chip, tp), device_id_type=MESH,
        )

    @pl.when(owner == core)
    def _():
        pltpu.make_async_copy(kvp_ref.at[my_slot], kv_buf.at[0], kv_recv.at[0]).start()

    def kv_start(i, _):
        @pl.when(target(i)[2] == core)
        def _():
            kv_copy(i).start()

        return 0

    lax.fori_loop(1, RING, kv_start, 0)

    def relay(i):
        return pltpu.make_async_remote_copy(
            src_ref=kv_buf.at[i], dst_ref=kv_buf.at[i],
            send_sem=relay_send.at[i], recv_sem=kv_recv.at[i],
            device_id=(pos, tp_base + 1 - core), device_id_type=MESH,
        )

    relays = (double == 0) & (owner == core)

    places = 8 + 8 * double
    chunks = 2 + 2 * double

    def unpack(s, _):
        pltpu.make_async_copy(q_buf.at[s], q_buf.at[s], q_recv.at[s]).wait()
        packed = q_buf[s].astype(jnp.float32)
        first = lanes((HALF, PAIR)) < HEAD_DIM
        q_all[s, :HALF] = jnp.where(first, packed, 0.0).astype(jnp.bfloat16)
        q_all[s, HALF:] = jnp.where(first, pltpu.roll(packed, HEAD_DIM, 1), 0.0).astype(jnp.bfloat16)
        return 0

    lax.fori_loop(0, places, unpack, 0)
    m_all[...] = jnp.full_like(m_all, -jnp.inf)
    acc_all[...] = jnp.zeros_like(acc_all)
    count = count_ref[lax.div(pos, RING)]

    def key_step(i, _):
        for n in range(2):
            slot = 2 * i + n
            pltpu.make_async_copy(kv_buf.at[slot], kv_buf.at[slot], kv_recv.at[slot]).wait()

            @pl.when(relays)
            def _():
                relay(slot).start()

        kv = kv_buf[pl.ds(2 * i, 2)].reshape(STEP, PAIR)
        lane = lanes((16, STEP))
        second = lane >= KEYS
        within = jnp.where(second, lane - KEYS, lane)
        rank = jnp.where(second, lax.rem(z + near(2 * i + 1), RING), lax.rem(z + near(2 * i), RING))
        live = (within >= IMG) | (rank * IMG + within < count)
        live = jnp.where(live, 1.0, 0.0).astype(jnp.bfloat16)
        value = jnp.concatenate([kv.T[HEAD_DIM:], live], axis=0)

        def chunk_step(j, _):
            q = q_all[pl.ds(4 * j, 4)].reshape(CHUNK, PAIR)
            s = lax.dot_general(
                kv, q, (((1,), (1,)), ((), ())), preferred_element_type=jnp.float32
            )
            m_old = m_all[j]
            m_new = jnp.maximum(m_old, jnp.max(s, axis=0, keepdims=True))
            p = jnp.exp2((s - m_new) * LOG2E).astype(jnp.bfloat16)
            decay = jnp.exp2((m_old - m_new) * LOG2E)
            acc_all[j] = acc_all[j] * decay + jnp.dot(value, p, preferred_element_type=jnp.float32)
            m_all[j] = m_new
            return 0

        lax.fori_loop(0, chunks, chunk_step, 0)
        return 0

    lax.fori_loop(0, RING // 2, key_step, 0)

    def home(s):
        return double * s + (1 - double) * (2 * s + core)

    def o_copy(s):
        return pltpu.make_async_remote_copy(
            src_ref=o_stage.at[s], dst_ref=o_buf.at[my_slot],
            send_sem=o_send.at[s], recv_sem=o_recv.at[my_slot],
            device_id=(base + home(s), tp_base + owner), device_id_type=MESH,
        )

    def stays(s):
        return (home(s) == z) & (owner == core)

    def finish(j, _):
        out = (acc_all[j, :HEAD_DIM] / acc_all[j, HEAD_DIM : HEAD_DIM + 1]).T
        for b in range(4):
            block = out[b * IMG : (b + 1) * IMG]
            both = jnp.concatenate([block[:HALF], block[HALF:]], axis=1)
            o_stage[4 * j + b] = both.astype(jnp.bfloat16)
        for b in range(4):
            s = 4 * j + b

            @pl.when(stays(s))
            def _():
                pltpu.make_async_copy(o_stage.at[s], o_buf.at[my_slot], o_recv.at[my_slot]).start()

            @pl.when(jnp.logical_not(stays(s)))
            def _():
                o_copy(s).start()

        return 0

    lax.fori_loop(0, chunks, finish, 0)

    limit = lax.div(HEADS + 3 - tp, 4)
    for j in range(SLOTS):
        pltpu.make_async_copy(o_buf.at[j], o_buf.at[j], o_recv.at[j]).wait()
        valid = jnp.where(j < limit, 1.0, 0.0)
        got = (o_buf[j].astype(jnp.float32) * valid).astype(jnp.bfloat16)
        columns = slice(j * HEAD_DIM, (j + 1) * HEAD_DIM)
        att_ref[:HALF, columns] = got[:, :HEAD_DIM]
        att_ref[HALF:, columns] = got[:, HEAD_DIM:]

    def drain(i, _):
        @pl.when(target(i)[2] == core)
        def _():
            q_copy(i).wait_send()
            kv_copy(i).wait_send()

        return 0

    lax.fori_loop(1, RING, drain, 0)

    @pl.when((owner == core) & jnp.logical_not(q_stays))
    def _():
        q_copy(0).wait_send()

    @pl.when(relays)
    def _():
        def relay_drain(i, _):
            relay(i).wait_send()
            return 0

        lax.fori_loop(0, RING, relay_drain, 0)

    def o_drain(s, _):
        @pl.when(jnp.logical_not(stays(s)))
        def _():
            o_copy(s).wait_send()

        return 0

    lax.fori_loop(0, places, o_drain, 0)


VMEM = pl.BlockSpec(memory_space=pltpu.VMEM)
SMEM = pl.BlockSpec(memory_space=pltpu.SMEM)


def local(query, keys, values, q_gain, k_gain, residual, gate, out_weight, image_count):
    bf16, f32 = jnp.bfloat16, jnp.float32
    q_packed, kv_packed = pl.pallas_call(
        prep_kernel,
        out_shape=(
            jax.ShapeDtypeStruct((SLOTS, HALF, PAIR), bf16),
            jax.ShapeDtypeStruct((SLOTS, KEYS, PAIR), bf16),
        ),
        in_specs=[SMEM] + [VMEM] * 5,
        out_specs=(VMEM, VMEM),
        name="prep",
    )(image_count, query, keys, values, q_gain.reshape(1, HEAD_DIM), k_gain)
    sem = pltpu.SemaphoreType.DMA
    attended = pl.pallas_call(
        main_kernel,
        out_shape=jax.ShapeDtypeStruct((IMG, SLOTS * HEAD_DIM), bf16),
        in_specs=[SMEM, VMEM, VMEM],
        out_specs=VMEM,
        scratch_shapes=[
            pltpu.VMEM((RING, KEYS, PAIR), bf16),
            pltpu.VMEM((RING, HALF, PAIR), bf16),
            pltpu.VMEM((RING, IMG, PAIR), bf16),
            pltpu.VMEM((4, 1, CHUNK), f32),
            pltpu.VMEM((4, HEAD_DIM + 16, CHUNK), f32),
            pltpu.VMEM((RING, HALF, PAIR), bf16),
            pltpu.VMEM((SLOTS, HALF, PAIR), bf16),
            sem((RING,)), sem((RING,)), sem((RING,)), sem((RING,)),
            sem((RING,)), sem((SLOTS,)), sem((RING,)),
        ],
        compiler_params=pltpu.CompilerParams(
            collective_id=0, has_side_effects=True, vmem_limit_bytes=48 * 2**20
        ),
        name="attend",
    )(image_count, q_packed, kv_packed)
    request = lax.axis_index("seq") // RING
    share = lax.psum_scatter(
        lax.dot_general(
            out_weight, attended, (((0,), (1,)), ((), ())), preferred_element_type=f32
        ).astype(bf16),
        "tp",
        scatter_dimension=0,
        tiled=True,
    ).astype(f32)
    projected = jnp.transpose(share)
    gate_row = lax.dynamic_index_in_dim(gate, request, 0, keepdims=False).astype(f32)
    return (residual.astype(f32) + gate_row[None, :] * projected).astype(bf16)


def solution(mesh):
    placed = (
        P("seq", "tp"),
        P("seq", "tp"),
        P("seq", "tp"),
        P(),
        P(),
        P("seq", "tp"),
        P(None, "tp"),
        P("tp", None),
        P(),
    )
    return jax.shard_map(
        local, mesh=mesh, in_specs=placed, out_specs=P("seq", "tp"), check_vma=False
    )
```

```python
import jax
import jax.numpy as jnp
from jax import lax
from jax.experimental import pallas as pl
from jax.experimental.pallas import tpu as pltpu
from jax.sharding import PartitionSpec as P

HEADS = 38
HEAD_DIM = 64
RING = 16
SLOTS = 10
IMG = 192
KEYS = 224
HALF = IMG // 2
PAIR = 2 * HEAD_DIM
CHUNK = 4 * IMG
STEP = 2 * KEYS
WIDE = 608
BLOCKS = 2
ROWS = IMG // BLOCKS
LOG2E = 1.4426950408889634
MESH = pl.DeviceIdType.MESH
epsilon = 1e-06


def lanes(shape):
    return lax.broadcasted_iota(jnp.int32, shape, 1)


def pack(low, high):
    first = lanes(low.shape) < HEAD_DIM
    even = jnp.where(first, low, pltpu.roll(high, HEAD_DIM, 1))
    odd = jnp.where(first, pltpu.roll(low, HEAD_DIM, 1), high)
    return even.astype(jnp.bfloat16), odd.astype(jnp.bfloat16)


def normed(value, gain, ones):
    x = value.astype(jnp.float32)
    square = x * x
    high = square.astype(jnp.bfloat16)
    low = (square - high.astype(jnp.float32)).astype(jnp.bfloat16)
    total = jnp.dot(high, ones, preferred_element_type=jnp.float32)
    total += jnp.dot(low, ones, preferred_element_type=jnp.float32)
    inverse = lax.rsqrt(total * (1.0 / HEAD_DIM) + epsilon)
    return (x * inverse * gain).astype(jnp.bfloat16).astype(jnp.float32)


def ones_pair():
    row = lax.broadcasted_iota(jnp.int32, (PAIR, PAIR), 0) < HEAD_DIM
    column = lanes((PAIR, PAIR)) < HEAD_DIM
    return jnp.where(row == column, 1.0, 0.0).astype(jnp.bfloat16)


def pack_queries(q_ref, qg_ref, qp_ref):
    gain = jnp.concatenate([qg_ref[...], qg_ref[...]], axis=1)
    ones = ones_pair()
    for p in range(SLOTS // 2):
        q = normed(q_ref[:, p * PAIR : (p + 1) * PAIR], gain, ones) * HEAD_DIM ** (-0.5)
        qp_ref[2 * p], qp_ref[2 * p + 1] = pack(q[:HALF], q[HALF:])


def pack_keys(left, k_ref, v_ref, kg_ref, kvp_ref):
    gain = jnp.concatenate([kg_ref[...], kg_ref[...]], axis=1)
    ones = ones_pair()
    key_row = lax.broadcasted_iota(jnp.int32, (KEYS, PAIR), 0)
    gain_rows = jnp.where(key_row < IMG, gain[0:1], gain[1:2])
    dead = (key_row < IMG) & (key_row >= left)
    for p in range(SLOTS // 2):
        columns = slice(p * PAIR, (p + 1) * PAIR)
        k = normed(k_ref[:, columns], gain_rows, ones)
        k = jnp.where(dead, k[IMG : IMG + 1], k)
        v = jnp.where(dead, 0.0, v_ref[:, columns].astype(jnp.float32))
        kvp_ref[2 * p], kvp_ref[2 * p + 1] = pack(k, v)


def near(i):
    return RING + (2 * lax.rem(i, 2) - 1) * lax.div(i + 1, 2)


def role(z, core):
    part, quarter = lax.rem(z, 4), lax.div(z, 4)
    double = lax.div(4 - part, 4)
    odd = lax.rem(part, 2)
    middle = (1 - double) * (1 - odd)
    owner = double * core + odd * lax.div(part, 2) + middle * lax.rem(quarter, 2)
    slot = double * quarter + odd * (4 + quarter) + middle * (8 + lax.div(z, 8))
    return double, owner, slot


def main_kernel(
    count_ref, q_hbm, k_hbm, v_hbm, qg_ref, kg_ref, res_hbm, gate_ref, w_hbm, out_ref,
    q_in, k_in, v_in, res_in, w_in, qp_ref, kvp_ref,
    kv_buf, q_buf, q_all, m_all, acc_all, o_stage, o_buf, att_ref,
    part, pair_in, mate_out, mate_in, load,
    kv_send, kv_recv, q_send, q_recv, o_send, o_recv, relay_send,
    pair_send, pair_recv, mate_send, mate_recv,
):
    pos = lax.axis_index("seq")
    tp = lax.axis_index("tp")
    z = lax.rem(pos, RING)
    base = pos - z
    core = lax.rem(tp, 2)
    tp_base = tp - core
    double, owner, my_slot = role(z, core)
    parity = lax.rem(z, 2)
    side = lax.div(tp, 2)
    mate = (pos, 2 * (1 - side) + core)
    sibling = (pos, tp_base + 1 - core)

    loads = [
        pltpu.make_async_copy(source, place, load.at[n])
        for n, (source, place) in enumerate(
            [(q_hbm, q_in), (k_hbm, k_in), (v_hbm, v_in), (res_hbm, res_in), (w_hbm, w_in)]
        )
    ]
    for copy in loads:
        copy.start()

    barrier = pltpu.get_barrier_semaphore()
    linear = z * 2 + core

    def greet(i, _):
        peer = lax.rem(linear + i, 2 * RING)
        pl.semaphore_signal(
            barrier,
            inc=1,
            device_id=(base + lax.div(peer, 2), tp_base + lax.rem(peer, 2)),
            device_id_type=MESH,
        )
        return 0

    lax.fori_loop(1, 2 * RING, greet, 0)
    pl.semaphore_signal(barrier, inc=1, device_id=mate, device_id_type=MESH)
    count = count_ref[lax.div(pos, RING)]
    loads[0].wait()
    pack_queries(q_in, qg_ref, qp_ref)
    loads[1].wait()
    loads[2].wait()
    pack_keys(count - z * IMG, k_in, v_in, kg_ref, kvp_ref)
    pl.semaphore_wait(barrier, 2 * RING)

    def target(i):
        chip = lax.rem(z + 2 * RING - near(i), RING)
        return (chip,) + role(chip, core)

    def q_copy(i):
        chip, dbl, _, slot = target(i)
        to_core = dbl * core + (1 - dbl) * parity
        place = dbl * z + (1 - dbl) * lax.div(z, 2)
        return pltpu.make_async_remote_copy(
            src_ref=qp_ref.at[slot], dst_ref=q_buf.at[place],
            send_sem=q_send.at[i], recv_sem=q_recv.at[place],
            device_id=(base + chip, tp_base + to_core), device_id_type=MESH,
        )

    q_local = double * z + (1 - double) * lax.div(z, 2)
    q_stays = (owner == core) & ((double == 1) | (parity == core))

    def q_start(k, _):
        i = RING - 1 - k

        @pl.when(target(i)[2] == core)
        def _():
            q_copy(i).start()

        return 0

    lax.fori_loop(0, RING - 1, q_start, 0)

    @pl.when(q_stays)
    def _():
        pltpu.make_async_copy(qp_ref.at[my_slot], q_buf.at[q_local], q_recv.at[q_local]).start()

    @pl.when((owner == core) & jnp.logical_not(q_stays))
    def _():
        q_copy(0).start()

    def kv_copy(i):
        chip, _, _, slot = target(i)
        return pltpu.make_async_remote_copy(
            src_ref=kvp_ref.at[slot], dst_ref=kv_buf.at[i],
            send_sem=kv_send.at[i], recv_sem=kv_recv.at[i],
            device_id=(base + chip, tp), device_id_type=MESH,
        )

    @pl.when(owner == core)
    def _():
        pltpu.make_async_copy(kvp_ref.at[my_slot], kv_buf.at[0], kv_recv.at[0]).start()

    def kv_start(i, _):
        @pl.when(target(i)[2] == core)
        def _():
            kv_copy(i).start()

        return 0

    lax.fori_loop(1, RING, kv_start, 0)

    def relay(i):
        return pltpu.make_async_remote_copy(
            src_ref=kv_buf.at[i], dst_ref=kv_buf.at[i],
            send_sem=relay_send.at[i], recv_sem=kv_recv.at[i],
            device_id=sibling, device_id_type=MESH,
        )

    relays = (double == 0) & (owner == core)

    places = 8 + 8 * double
    chunks = 2 + 2 * double

    def unpack(s, _):
        pltpu.make_async_copy(q_buf.at[s], q_buf.at[s], q_recv.at[s]).wait()
        packed = q_buf[s].astype(jnp.float32)
        first = lanes((HALF, PAIR)) < HEAD_DIM
        q_all[s, :HALF] = jnp.where(first, packed, 0.0).astype(jnp.bfloat16)
        q_all[s, HALF:] = jnp.where(first, pltpu.roll(packed, HEAD_DIM, 1), 0.0).astype(jnp.bfloat16)
        return 0

    lax.fori_loop(0, places, unpack, 0)
    m_all[...] = jnp.full_like(m_all, -jnp.inf)
    acc_all[...] = jnp.zeros_like(acc_all)

    def key_step(i, _):
        for n in range(2):
            slot = 2 * i + n
            pltpu.make_async_copy(kv_buf.at[slot], kv_buf.at[slot], kv_recv.at[slot]).wait()

            @pl.when(relays)
            def _():
                relay(slot).start()

        kv = kv_buf[pl.ds(2 * i, 2)].reshape(STEP, PAIR)
        lane = lanes((16, STEP))
        second = lane >= KEYS
        within = jnp.where(second, lane - KEYS, lane)
        rank = jnp.where(second, lax.rem(z + near(2 * i + 1), RING), lax.rem(z + near(2 * i), RING))
        live = (within >= IMG) | (rank * IMG + within < count)
        live = jnp.where(live, 1.0, 0.0).astype(jnp.bfloat16)
        value = jnp.concatenate([kv.T[HEAD_DIM:], live], axis=0)

        def chunk_step(j, _):
            q = q_all[pl.ds(4 * j, 4)].reshape(CHUNK, PAIR)
            s = lax.dot_general(
                kv, q, (((1,), (1,)), ((), ())), preferred_element_type=jnp.float32
            )
            m_old = m_all[j]
            m_new = jnp.maximum(m_old, jnp.max(s, axis=0, keepdims=True))
            p = jnp.exp2((s - m_new) * LOG2E).astype(jnp.bfloat16)
            decay = jnp.exp2((m_old - m_new) * LOG2E)
            acc_all[j] = acc_all[j] * decay + jnp.dot(value, p, preferred_element_type=jnp.float32)
            m_all[j] = m_new
            return 0

        lax.fori_loop(0, chunks, chunk_step, 0)
        return 0

    lax.fori_loop(0, RING // 2, key_step, 0)

    def home(s):
        return double * s + (1 - double) * (2 * s + core)

    def o_copy(s):
        return pltpu.make_async_remote_copy(
            src_ref=o_stage.at[s], dst_ref=o_buf.at[my_slot],
            send_sem=o_send.at[s], recv_sem=o_recv.at[my_slot],
            device_id=(base + home(s), tp_base + owner), device_id_type=MESH,
        )

    def stays(s):
        return (home(s) == z) & (owner == core)

    def finish(j, _):
        out = (acc_all[j, :HEAD_DIM] / acc_all[j, HEAD_DIM : HEAD_DIM + 1]).T
        for b in range(4):
            block = out[b * IMG : (b + 1) * IMG]
            both = jnp.concatenate([block[:HALF], block[HALF:]], axis=1)
            o_stage[4 * j + b] = both.astype(jnp.bfloat16)
        for b in range(4):
            s = 4 * j + b

            @pl.when(stays(s))
            def _():
                pltpu.make_async_copy(o_stage.at[s], o_buf.at[my_slot], o_recv.at[my_slot]).start()

            @pl.when(jnp.logical_not(stays(s)))
            def _():
                o_copy(s).start()

        return 0

    lax.fori_loop(0, chunks, finish, 0)

    limit = lax.div(HEADS + 3 - tp, 4)
    for j in range(SLOTS):
        pltpu.make_async_copy(o_buf.at[j], o_buf.at[j], o_recv.at[j]).wait()
        valid = jnp.where(j < limit, 1.0, 0.0)
        got = (o_buf[j].astype(jnp.float32) * valid).astype(jnp.bfloat16)
        columns = slice(j * HEAD_DIM, (j + 1) * HEAD_DIM)
        att_ref[:HALF, columns] = got[:, :HEAD_DIM]
        att_ref[HALF:, columns] = got[:, HEAD_DIM:]

    def pair_copy(n):
        return pltpu.make_async_remote_copy(
            src_ref=part.at[n, 1 - core], dst_ref=pair_in.at[n],
            send_sem=pair_send.at[n], recv_sem=pair_recv.at[n],
            device_id=sibling, device_id_type=MESH,
        )

    def mate_copy(n):
        return pltpu.make_async_remote_copy(
            src_ref=mate_out.at[n], dst_ref=mate_in.at[n],
            send_sem=mate_send.at[n], recv_sem=mate_recv.at[n],
            device_id=mate, device_id_type=MESH,
        )

    loads[4].wait()
    for n in range(BLOCKS):
        product = jnp.dot(
            att_ref[n * ROWS : (n + 1) * ROWS], w_in[...], preferred_element_type=jnp.float32
        ).astype(jnp.bfloat16)
        for t in range(4):
            part[n, t % 2, t // 2] = product[:, t * WIDE : (t + 1) * WIDE]
        pair_copy(n).start()
    for n in range(BLOCKS):
        pair_copy(n).wait_recv()
        both = part[n, core, 1 - side].astype(jnp.float32) + pair_in[n, 1 - side].astype(jnp.float32)
        mate_out[n] = both.astype(jnp.bfloat16)
        mate_copy(n).start()
    loads[3].wait()
    gates = gate_ref[...].astype(jnp.float32)
    chosen = lax.broadcasted_iota(jnp.int32, gates.shape, 0) == lax.div(pos, RING)
    gate_row = jnp.sum(jnp.where(chosen, gates, 0.0), axis=0, keepdims=True)
    for n in range(BLOCKS):
        rows = slice(n * ROWS, (n + 1) * ROWS)
        both = part[n, core, side].astype(jnp.float32) + pair_in[n, side].astype(jnp.float32)
        mate_copy(n).wait_recv()
        projected = both + mate_in[n].astype(jnp.float32)
        updated = res_in[rows].astype(jnp.float32) + gate_row * projected
        out_ref[rows] = updated.astype(jnp.bfloat16)
    for n in range(BLOCKS):
        pair_copy(n).wait_send()
        mate_copy(n).wait_send()

    def drain(i, _):
        @pl.when(target(i)[2] == core)
        def _():
            q_copy(i).wait_send()
            kv_copy(i).wait_send()

        return 0

    lax.fori_loop(1, RING, drain, 0)

    @pl.when((owner == core) & jnp.logical_not(q_stays))
    def _():
        q_copy(0).wait_send()

    @pl.when(relays)
    def _():
        def relay_drain(i, _):
            relay(i).wait_send()
            return 0

        lax.fori_loop(0, RING, relay_drain, 0)

    def o_drain(s, _):
        @pl.when(jnp.logical_not(stays(s)))
        def _():
            o_copy(s).wait_send()

        return 0

    lax.fori_loop(0, places, o_drain, 0)


VMEM = pl.BlockSpec(memory_space=pltpu.VMEM)
SMEM = pl.BlockSpec(memory_space=pltpu.SMEM)
HBM = pl.BlockSpec(memory_space=pltpu.HBM)


def local(query, keys, values, q_gain, k_gain, residual, gate, out_weight, image_count):
    bf16, f32 = jnp.bfloat16, jnp.float32
    sem = pltpu.SemaphoreType.DMA
    return pl.pallas_call(
        main_kernel,
        out_shape=jax.ShapeDtypeStruct(residual.shape, bf16),
        in_specs=[SMEM, HBM, HBM, HBM, VMEM, VMEM, HBM, VMEM, HBM],
        out_specs=VMEM,
        scratch_shapes=[
            pltpu.VMEM(query.shape, bf16),
            pltpu.VMEM(keys.shape, bf16),
            pltpu.VMEM(values.shape, bf16),
            pltpu.VMEM(residual.shape, bf16),
            pltpu.VMEM(out_weight.shape, bf16),
            pltpu.VMEM((SLOTS, HALF, PAIR), bf16),
            pltpu.VMEM((SLOTS, KEYS, PAIR), bf16),
            pltpu.VMEM((RING, KEYS, PAIR), bf16),
            pltpu.VMEM((RING, HALF, PAIR), bf16),
            pltpu.VMEM((RING, IMG, PAIR), bf16),
            pltpu.VMEM((4, 1, CHUNK), f32),
            pltpu.VMEM((4, HEAD_DIM + 16, CHUNK), f32),
            pltpu.VMEM((RING, HALF, PAIR), bf16),
            pltpu.VMEM((SLOTS, HALF, PAIR), bf16),
            pltpu.VMEM((IMG, SLOTS * HEAD_DIM), bf16),
            pltpu.VMEM((BLOCKS, 2, 2, ROWS, WIDE), bf16),
            pltpu.VMEM((BLOCKS, 2, ROWS, WIDE), bf16),
            pltpu.VMEM((BLOCKS, ROWS, WIDE), bf16),
            pltpu.VMEM((BLOCKS, ROWS, WIDE), bf16),
            sem((5,)),
            sem((RING,)), sem((RING,)), sem((RING,)), sem((RING,)),
            sem((RING,)), sem((SLOTS,)), sem((RING,)),
            sem((BLOCKS,)), sem((BLOCKS,)), sem((BLOCKS,)), sem((BLOCKS,)),
        ],
        compiler_params=pltpu.CompilerParams(
            collective_id=0, has_side_effects=True, vmem_limit_bytes=65_000_000
        ),
        name="attend",
    )(
        image_count, query, keys, values, q_gain.reshape(1, HEAD_DIM), k_gain,
        residual, gate, out_weight,
    )


def solution(mesh):
    placed = (
        P("seq", "tp"),
        P("seq", "tp"),
        P("seq", "tp"),
        P(),
        P(),
        P("seq", "tp"),
        P(None, "tp"),
        P("tp", None),
        P(),
    )
    return jax.shard_map(
        local, mesh=mesh, in_specs=placed, out_specs=P("seq", "tp"), check_vma=False
    )
```

```python
import jax
import jax.numpy as jnp
from jax import lax
from jax.experimental import pallas as pl
from jax.experimental.pallas import tpu as pltpu
from jax.sharding import PartitionSpec as P

HEADS = 38
HEAD_DIM = 64
RING = 16
SLOTS = 10
IMG = 192
KEYS = 224
HALF = IMG // 2
PAIR = 2 * HEAD_DIM
GROUP = 8
CHUNK = GROUP * IMG
STEP = 2 * KEYS
WIDE = 608
BLOCKS = 4
ROWS = IMG // BLOCKS
LOG2E = 1.4426950408889634
MESH = pl.DeviceIdType.MESH
epsilon = 1e-06


def lanes(shape):
    return lax.broadcasted_iota(jnp.int32, shape, 1)


def pack(low, high):
    first = lanes(low.shape) < HEAD_DIM
    even = jnp.where(first, low, pltpu.roll(high, HEAD_DIM, 1))
    odd = jnp.where(first, pltpu.roll(low, HEAD_DIM, 1), high)
    return even.astype(jnp.bfloat16), odd.astype(jnp.bfloat16)


def normed(value, gain, ones):
    x = value.astype(jnp.float32)
    square = x * x
    high = square.astype(jnp.bfloat16)
    low = (square - high.astype(jnp.float32)).astype(jnp.bfloat16)
    total = jnp.dot(high, ones, preferred_element_type=jnp.float32)
    total += jnp.dot(low, ones, preferred_element_type=jnp.float32)
    inverse = lax.rsqrt(total * (1.0 / HEAD_DIM) + epsilon)
    return (x * inverse * gain).astype(jnp.bfloat16).astype(jnp.float32)


def ones_pair():
    row = lax.broadcasted_iota(jnp.int32, (PAIR, PAIR), 0) < HEAD_DIM
    column = lanes((PAIR, PAIR)) < HEAD_DIM
    return jnp.where(row == column, 1.0, 0.0).astype(jnp.bfloat16)


def pack_queries(q_ref, qg_ref, qp_ref):
    gain = jnp.concatenate([qg_ref[...], qg_ref[...]], axis=1)
    ones = ones_pair()
    for p in range(SLOTS // 2):
        q = normed(q_ref[:, p * PAIR : (p + 1) * PAIR], gain, ones) * HEAD_DIM ** (-0.5)
        qp_ref[2 * p], qp_ref[2 * p + 1] = pack(q[:HALF], q[HALF:])


def pack_keys(left, k_ref, v_ref, kg_ref, kvp_ref):
    gain = jnp.concatenate([kg_ref[...], kg_ref[...]], axis=1)
    ones = ones_pair()
    key_row = lax.broadcasted_iota(jnp.int32, (KEYS, PAIR), 0)
    gain_rows = jnp.where(key_row < IMG, gain[0:1], gain[1:2])
    dead = (key_row < IMG) & (key_row >= left)
    for p in range(SLOTS // 2):
        columns = slice(p * PAIR, (p + 1) * PAIR)
        k = normed(k_ref[:, columns], gain_rows, ones)
        k = jnp.where(dead, k[IMG : IMG + 1], k)
        v = jnp.where(dead, 0.0, v_ref[:, columns].astype(jnp.float32))
        kvp_ref[2 * p], kvp_ref[2 * p + 1] = pack(k, v)


def near(i):
    return RING + (2 * lax.rem(i, 2) - 1) * lax.div(i + 1, 2)


def role(z, core):
    part, quarter = lax.rem(z, 4), lax.div(z, 4)
    double = lax.div(4 - part, 4)
    odd = lax.rem(part, 2)
    middle = (1 - double) * (1 - odd)
    owner = double * core + odd * lax.div(part, 2) + middle * lax.rem(quarter, 2)
    slot = double * quarter + odd * (4 + quarter) + middle * (8 + lax.div(z, 8))
    return double, owner, slot


def main_kernel(
    count_ref, q_hbm, k_hbm, v_hbm, qg_ref, kg_ref, res_hbm, gate_ref, w_hbm, out_ref,
    q_in, k_in, v_in, res_in, w_in, qp_ref, kvp_ref,
    kv_buf, q_buf, q_all, m_all, acc_all, o_stage, o_buf, att_ref,
    part, pair_in, mate_out, mate_in, load,
    kv_send, kv_recv, q_send, q_recv, o_send, o_recv, relay_send,
    pair_send, pair_recv, mate_send, mate_recv,
):
    pos = lax.axis_index("seq")
    tp = lax.axis_index("tp")
    z = lax.rem(pos, RING)
    base = pos - z
    core = lax.rem(tp, 2)
    tp_base = tp - core
    double, owner, my_slot = role(z, core)
    side = lax.div(tp, 2)
    mate = (pos, 2 * (1 - side) + core)
    sibling = (pos, tp_base + 1 - core)

    loads = [
        pltpu.make_async_copy(source, place, load.at[n])
        for n, (source, place) in enumerate(
            [(q_hbm, q_in), (k_hbm, k_in), (v_hbm, v_in), (res_hbm, res_in), (w_hbm, w_in)]
        )
    ]
    for copy in loads:
        copy.start()

    barrier = pltpu.get_barrier_semaphore()
    linear = z * 2 + core

    def greet(i, _):
        peer = lax.rem(linear + i, 2 * RING)
        pl.semaphore_signal(
            barrier,
            inc=1,
            device_id=(base + lax.div(peer, 2), tp_base + lax.rem(peer, 2)),
            device_id_type=MESH,
        )
        return 0

    lax.fori_loop(1, 2 * RING, greet, 0)
    pl.semaphore_signal(barrier, inc=1, device_id=mate, device_id_type=MESH)
    count = count_ref[lax.div(pos, RING)]
    loads[0].wait()
    pack_queries(q_in, qg_ref, qp_ref)
    pl.semaphore_wait(barrier, 2 * RING)

    def target(i):
        chip = lax.rem(z + 2 * RING - near(i), RING)
        return (chip,) + role(chip, core)

    def q_copy(i):
        chip, dbl, _, slot = target(i)
        to_core = dbl * core + (1 - dbl) * lax.rem(lax.div(i, 2), 2)
        place = dbl * i + (1 - dbl) * (2 * lax.div(i, 4) + lax.rem(i, 2))
        return pltpu.make_async_remote_copy(
            src_ref=qp_ref.at[slot], dst_ref=q_buf.at[place],
            send_sem=q_send.at[i], recv_sem=q_recv.at[place],
            device_id=(base + chip, tp_base + to_core), device_id_type=MESH,
        )

    q_stays = (owner == core) & ((double == 1) | (core == 0))

    def q_pass(kind):
        def q_start(k, _):
            i = RING - 1 - k
            _, dbl, own, _ = target(i)

            @pl.when((own == core) & (dbl == kind))
            def _():
                q_copy(i).start()

            return 0

        lax.fori_loop(0, RING - 1, q_start, 0)

    def kv_pass(kind):
        def kv_start(i, _):
            _, dbl, own, _ = target(i)

            @pl.when((own == core) & (dbl == kind))
            def _():
                kv_copy(i).start()

            return 0

        lax.fori_loop(1, RING, kv_start, 0)

    q_pass(1)
    @pl.when(q_stays)
    def _():
        pltpu.make_async_copy(qp_ref.at[my_slot], q_buf.at[0], q_recv.at[0]).start()

    @pl.when((owner == core) & jnp.logical_not(q_stays))
    def _():
        q_copy(0).start()

    loads[1].wait()
    loads[2].wait()
    pack_keys(count - z * IMG, k_in, v_in, kg_ref, kvp_ref)

    def kv_copy(i):
        chip, _, _, slot = target(i)
        return pltpu.make_async_remote_copy(
            src_ref=kvp_ref.at[slot], dst_ref=kv_buf.at[i],
            send_sem=kv_send.at[i], recv_sem=kv_recv.at[i],
            device_id=(base + chip, tp), device_id_type=MESH,
        )

    @pl.when(owner == core)
    def _():
        pltpu.make_async_copy(kvp_ref.at[my_slot], kv_buf.at[0], kv_recv.at[0]).start()

    kv_pass(1)
    q_pass(0)
    kv_pass(0)

    def relay(i):
        return pltpu.make_async_remote_copy(
            src_ref=kv_buf.at[i], dst_ref=kv_buf.at[i],
            send_sem=relay_send.at[i], recv_sem=kv_recv.at[i],
            device_id=sibling, device_id_type=MESH,
        )

    relays = (double == 0) & (owner == core)

    places = 8 + 8 * double
    chunks = 1 + double

    def unpack(s, _):
        pltpu.make_async_copy(q_buf.at[s], q_buf.at[s], q_recv.at[s]).wait()
        packed = q_buf[s].astype(jnp.float32)
        first = lanes((HALF, PAIR)) < HEAD_DIM
        q_all[s, :HALF] = jnp.where(first, packed, 0.0).astype(jnp.bfloat16)
        q_all[s, HALF:] = jnp.where(first, pltpu.roll(packed, HEAD_DIM, 1), 0.0).astype(jnp.bfloat16)
        return 0

    lax.fori_loop(0, places, unpack, 0)
    m_all[...] = jnp.full_like(m_all, -jnp.inf)
    acc_all[...] = jnp.zeros_like(acc_all)

    def arrive(i):
        for n in range(2):
            slot = 2 * i + n
            pltpu.make_async_copy(kv_buf.at[slot], kv_buf.at[slot], kv_recv.at[slot]).wait()

            @pl.when(relays)
            def _():
                relay(slot).start()

        kv = kv_buf[pl.ds(2 * i, 2)].reshape(STEP, PAIR)
        lane = lanes((16, STEP))
        second = lane >= KEYS
        within = jnp.where(second, lane - KEYS, lane)
        rank = jnp.where(second, lax.rem(z + near(2 * i + 1), RING), lax.rem(z + near(2 * i), RING))
        live = (within >= IMG) | (rank * IMG + within < count)
        live = jnp.where(live, 1.0, 0.0).astype(jnp.bfloat16)
        value = jnp.concatenate([kv.T[HEAD_DIM:], live], axis=0)

        return kv, value

    def chunk_step(kv, value, j):
        q = q_all[pl.ds(GROUP * j, GROUP)].reshape(CHUNK, PAIR)
        s = lax.dot_general(kv, q, (((1,), (1,)), ((), ())), preferred_element_type=jnp.float32)
        m_old = m_all[j]
        m_new = jnp.maximum(m_old, jnp.max(s, axis=0, keepdims=True))
        p = jnp.exp2((s - m_new) * LOG2E).astype(jnp.bfloat16)
        decay = jnp.exp2((m_old - m_new) * LOG2E)
        acc_all[j] = acc_all[j] * decay + jnp.dot(value, p, preferred_element_type=jnp.float32)
        m_all[j] = m_new

    def key_step(i, _):
        kv, value = arrive(i)

        def each(j, _):
            chunk_step(kv, value, j)
            return 0

        lax.fori_loop(0, chunks, each, 0)
        return 0

    lax.fori_loop(0, RING // 2 - 1, key_step, 0)

    def home(s):
        i = double * s + (1 - double) * (4 * lax.div(s, 2) + 2 * core + lax.rem(s, 2))
        return lax.rem(z + near(i), RING)

    def o_copy(s, n):
        return pltpu.make_async_remote_copy(
            src_ref=o_stage.at[s, n], dst_ref=o_buf.at[my_slot, n],
            send_sem=o_send.at[s, n], recv_sem=o_recv.at[my_slot, n],
            device_id=(base + home(s), tp_base + owner), device_id_type=MESH,
        )

    def stays(s):
        return (home(s) == z) & (owner == core)

    def o_start(s, n):
        @pl.when(stays(s))
        def _():
            pltpu.make_async_copy(
                o_stage.at[s, n], o_buf.at[my_slot, n], o_recv.at[my_slot, n]
            ).start()

        @pl.when(jnp.logical_not(stays(s)))
        def _():
            o_copy(s, n).start()

    def finish(j):
        out = (acc_all[j, :HEAD_DIM] / acc_all[j, HEAD_DIM : HEAD_DIM + 1]).T
        for b in range(GROUP):
            for n in range(2):
                at = b * IMG + n * HALF
                both = jnp.concatenate([out[at : at + ROWS], out[at + ROWS : at + HALF]], axis=1)
                o_stage[GROUP * j + b, n] = both.astype(jnp.bfloat16)
        for b in range(GROUP - 1, -1, -1):
            o_start(GROUP * j + b, 0)

    kv_last, value_last = arrive(RING // 2 - 1)

    def last_chunks(k, _):
        j = chunks - 1 - k
        chunk_step(kv_last, value_last, j)
        finish(j)
        return 0

    lax.fori_loop(0, chunks, last_chunks, 0)

    def o_rest(k, _):
        o_start(places - 1 - k, 1)
        return 0

    lax.fori_loop(0, places, o_rest, 0)
    limit = lax.div(HEADS + 3 - tp, 4)

    def gather(n):
        for j in range(SLOTS):
            pltpu.make_async_copy(o_buf.at[j, n], o_buf.at[j, n], o_recv.at[j, n]).wait()
            valid = jnp.where(j < limit, 1.0, 0.0)
            got = (o_buf[j, n].astype(jnp.float32) * valid).astype(jnp.bfloat16)
            columns = slice(j * HEAD_DIM, (j + 1) * HEAD_DIM)
            att_ref[n * HALF : n * HALF + ROWS, columns] = got[:, :HEAD_DIM]
            att_ref[n * HALF + ROWS : (n + 1) * HALF, columns] = got[:, HEAD_DIM:]

    def pair_copy(n):
        return pltpu.make_async_remote_copy(
            src_ref=part.at[n, 1 - core], dst_ref=pair_in.at[n],
            send_sem=pair_send.at[n], recv_sem=pair_recv.at[n],
            device_id=sibling, device_id_type=MESH,
        )

    def mate_copy(n):
        return pltpu.make_async_remote_copy(
            src_ref=mate_out.at[n], dst_ref=mate_in.at[n],
            send_sem=mate_send.at[n], recv_sem=mate_recv.at[n],
            device_id=mate, device_id_type=MESH,
        )

    loads[4].wait()
    loads[3].wait()
    gates = gate_ref[...].astype(jnp.float32)
    chosen = lax.broadcasted_iota(jnp.int32, gates.shape, 0) == lax.div(pos, RING)
    gate_row = jnp.sum(jnp.where(chosen, gates, 0.0), axis=0, keepdims=True)

    for half in range(2):
        gather(half)
        product = jnp.dot(
            att_ref[half * HALF : (half + 1) * HALF], w_in[...], preferred_element_type=jnp.float32
        ).astype(jnp.bfloat16)
        blocks = (2 * half, 2 * half + 1)
        for n in blocks:
            rows = slice((n % 2) * ROWS, (n % 2 + 1) * ROWS)
            for t in range(4):
                part[n, t % 2, t // 2] = product[rows, t * WIDE : (t + 1) * WIDE]
            pair_copy(n).start()
        for n in blocks:
            pair_copy(n).wait_recv()
            both = part[n, core, 1 - side].astype(jnp.float32)
            both += pair_in[n, 1 - side].astype(jnp.float32)
            mate_out[n] = both.astype(jnp.bfloat16)
            mate_copy(n).start()
    for n in range(BLOCKS):
        rows = slice(n * ROWS, (n + 1) * ROWS)
        both = part[n, core, side].astype(jnp.float32) + pair_in[n, side].astype(jnp.float32)
        mate_copy(n).wait_recv()
        projected = both + mate_in[n].astype(jnp.float32)
        updated = res_in[rows].astype(jnp.float32) + gate_row * projected
        out_ref[rows] = updated.astype(jnp.bfloat16)
    for n in range(BLOCKS):
        pair_copy(n).wait_send()
        mate_copy(n).wait_send()

    def drain(i, _):
        @pl.when(target(i)[2] == core)
        def _():
            q_copy(i).wait_send()
            kv_copy(i).wait_send()

        return 0

    lax.fori_loop(1, RING, drain, 0)

    @pl.when((owner == core) & jnp.logical_not(q_stays))
    def _():
        q_copy(0).wait_send()

    @pl.when(relays)
    def _():
        def relay_drain(i, _):
            relay(i).wait_send()
            return 0

        lax.fori_loop(0, RING, relay_drain, 0)

    def o_drain(s, _):
        @pl.when(jnp.logical_not(stays(s)))
        def _():
            o_copy(s, 0).wait_send()
            o_copy(s, 1).wait_send()

        return 0

    lax.fori_loop(0, places, o_drain, 0)


VMEM = pl.BlockSpec(memory_space=pltpu.VMEM)
SMEM = pl.BlockSpec(memory_space=pltpu.SMEM)
HBM = pl.BlockSpec(memory_space=pltpu.HBM)


def local(query, keys, values, q_gain, k_gain, residual, gate, out_weight, image_count):
    bf16, f32 = jnp.bfloat16, jnp.float32
    sem = pltpu.SemaphoreType.DMA
    return pl.pallas_call(
        main_kernel,
        out_shape=jax.ShapeDtypeStruct(residual.shape, bf16),
        in_specs=[SMEM, HBM, HBM, HBM, VMEM, VMEM, HBM, VMEM, HBM],
        out_specs=VMEM,
        scratch_shapes=[
            pltpu.VMEM(query.shape, bf16),
            pltpu.VMEM(keys.shape, bf16),
            pltpu.VMEM(values.shape, bf16),
            pltpu.VMEM(residual.shape, bf16),
            pltpu.VMEM(out_weight.shape, bf16),
            pltpu.VMEM((SLOTS, HALF, PAIR), bf16),
            pltpu.VMEM((SLOTS, KEYS, PAIR), bf16),
            pltpu.VMEM((RING, KEYS, PAIR), bf16),
            pltpu.VMEM((RING, HALF, PAIR), bf16),
            pltpu.VMEM((RING, IMG, PAIR), bf16),
            pltpu.VMEM((2, 1, CHUNK), f32),
            pltpu.VMEM((2, HEAD_DIM + 16, CHUNK), f32),
            pltpu.VMEM((RING, 2, ROWS, PAIR), bf16),
            pltpu.VMEM((SLOTS, 2, ROWS, PAIR), bf16),
            pltpu.VMEM((IMG, SLOTS * HEAD_DIM), bf16),
            pltpu.VMEM((BLOCKS, 2, 2, ROWS, WIDE), bf16),
            pltpu.VMEM((BLOCKS, 2, ROWS, WIDE), bf16),
            pltpu.VMEM((BLOCKS, ROWS, WIDE), bf16),
            pltpu.VMEM((BLOCKS, ROWS, WIDE), bf16),
            sem((5,)),
            sem((RING,)), sem((RING,)), sem((RING,)), sem((RING,)),
            sem((RING, 2)), sem((SLOTS, 2)), sem((RING,)),
            sem((BLOCKS,)), sem((BLOCKS,)), sem((BLOCKS,)), sem((BLOCKS,)),
        ],
        compiler_params=pltpu.CompilerParams(
            collective_id=0, has_side_effects=True, vmem_limit_bytes=65_000_000
        ),
        name="attend",
    )(
        image_count, query, keys, values, q_gain.reshape(1, HEAD_DIM), k_gain,
        residual, gate, out_weight,
    )


def solution(mesh):
    placed = (
        P("seq", "tp"),
        P("seq", "tp"),
        P("seq", "tp"),
        P(),
        P(),
        P("seq", "tp"),
        P(None, "tp"),
        P("tp", None),
        P(),
    )
    return jax.shard_map(
        local, mesh=mesh, in_specs=placed, out_specs=P("seq", "tp"), check_vma=False
    )
```

```python
import jax
import jax.numpy as jnp
from jax import lax
from jax.experimental import pallas as pl
from jax.experimental.pallas import tpu as pltpu
from jax.sharding import PartitionSpec as P

HEADS = 38
HEAD_DIM = 64
RING = 16
SLOTS = 10
IMG = 192
KEYS = 224
HALF = IMG // 2
PAIR = 2 * HEAD_DIM
GROUP = 8
CHUNK = GROUP * IMG
STEP = 2 * KEYS
WIDE = 608
BLOCKS = 3
ROWS = IMG // BLOCKS
PIECES = ((0, 64), (128, 32))
LOG2E = 1.4426950408889634
MESH = pl.DeviceIdType.MESH
epsilon = 1e-06


def lanes(shape):
    return lax.broadcasted_iota(jnp.int32, shape, 1)


def pack(low, high):
    first = lanes(low.shape) < HEAD_DIM
    even = jnp.where(first, low, pltpu.roll(high, HEAD_DIM, 1))
    odd = jnp.where(first, pltpu.roll(low, HEAD_DIM, 1), high)
    return even.astype(jnp.bfloat16), odd.astype(jnp.bfloat16)


def normed(value, gain, ones):
    x = value.astype(jnp.float32)
    square = x * x
    high = square.astype(jnp.bfloat16)
    low = (square - high.astype(jnp.float32)).astype(jnp.bfloat16)
    total = jnp.dot(high, ones, preferred_element_type=jnp.float32)
    total += jnp.dot(low, ones, preferred_element_type=jnp.float32)
    inverse = lax.rsqrt(total * (1.0 / HEAD_DIM) + epsilon)
    return (x * inverse * gain).astype(jnp.bfloat16).astype(jnp.float32)


def ones_pair():
    row = lax.broadcasted_iota(jnp.int32, (PAIR, PAIR), 0) < HEAD_DIM
    column = lanes((PAIR, PAIR)) < HEAD_DIM
    return jnp.where(row == column, 1.0, 0.0).astype(jnp.bfloat16)


def pack_queries(q_ref, qg_ref, qp_ref):
    gain = jnp.concatenate([qg_ref[...], qg_ref[...]], axis=1)
    ones = ones_pair()
    for p in range(SLOTS // 2):
        q = normed(q_ref[:, p * PAIR : (p + 1) * PAIR], gain, ones) * HEAD_DIM ** (-0.5)
        qp_ref[2 * p], qp_ref[2 * p + 1] = pack(q[:HALF], q[HALF:])


def pack_keys(left, k_ref, v_ref, kg_ref, kvp_ref):
    gain = jnp.concatenate([kg_ref[...], kg_ref[...]], axis=1)
    ones = ones_pair()
    key_row = lax.broadcasted_iota(jnp.int32, (KEYS, PAIR), 0)
    gain_rows = jnp.where(key_row < IMG, gain[0:1], gain[1:2])
    dead = (key_row < IMG) & (key_row >= left)
    for p in range(SLOTS // 2):
        columns = slice(p * PAIR, (p + 1) * PAIR)
        k = normed(k_ref[:, columns], gain_rows, ones)
        k = jnp.where(dead, k[IMG : IMG + 1], k)
        v = jnp.where(dead, 0.0, v_ref[:, columns].astype(jnp.float32))
        kvp_ref[2 * p], kvp_ref[2 * p + 1] = pack(k, v)


def near(i):
    return RING + (2 * lax.rem(i, 2) - 1) * lax.div(i + 1, 2)


def role(z, core):
    part, quarter = lax.rem(z, 4), lax.div(z, 4)
    double = lax.div(4 - part, 4)
    odd = lax.rem(part, 2)
    middle = (1 - double) * (1 - odd)
    owner = double * core + odd * lax.div(part, 2) + middle * lax.rem(quarter, 2)
    slot = double * quarter + odd * (4 + quarter) + middle * (8 + lax.div(z, 8))
    return double, owner, slot


def main_kernel(
    count_ref, q_hbm, k_hbm, v_hbm, qg_ref, kg_ref, res_hbm, gate_ref, w_hbm, out_ref,
    q_in, k_in, v_in, res_in, w_in, qp_ref, kvp_ref,
    kv_buf, q_buf, q_all, m_all, acc_all,
    o_stage_a, o_stage_b, o_buf_a, o_buf_b, att_ref,
    part, pair_in, mate_out, mate_in, load,
    kv_send, kv_recv, q_send, q_recv, o_send, o_recv, relay_send,
    pair_send, pair_recv, mate_send, mate_recv,
):
    o_stage, o_buf = (o_stage_a, o_stage_b), (o_buf_a, o_buf_b)
    pos = lax.axis_index("seq")
    tp = lax.axis_index("tp")
    z = lax.rem(pos, RING)
    base = pos - z
    core = lax.rem(tp, 2)
    tp_base = tp - core
    double, owner, my_slot = role(z, core)
    side = lax.div(tp, 2)
    mate = (pos, 2 * (1 - side) + core)
    sibling = (pos, tp_base + 1 - core)

    barrier = pltpu.get_barrier_semaphore()
    linear = z * 2 + core

    def greet(i, _):
        peer = lax.rem(linear + i, 2 * RING)
        pl.semaphore_signal(
            barrier,
            inc=1,
            device_id=(base + lax.div(peer, 2), tp_base + lax.rem(peer, 2)),
            device_id_type=MESH,
        )
        return 0

    for low, high in ((8, 25), (1, 8), (25, 32)):
        lax.fori_loop(low, high, greet, 0)
    pl.semaphore_signal(barrier, inc=1, device_id=mate, device_id_type=MESH)
    loads = [
        pltpu.make_async_copy(source, place, load.at[n])
        for n, (source, place) in enumerate(
            [(q_hbm, q_in), (k_hbm, k_in), (v_hbm, v_in), (res_hbm, res_in), (w_hbm, w_in)]
        )
    ]
    for copy in loads:
        copy.start()

    count = count_ref[lax.div(pos, RING)]
    loads[0].wait()
    pack_queries(q_in, qg_ref, qp_ref)
    pl.semaphore_wait(barrier, 2 * RING)

    def target(i):
        chip = lax.rem(z + 2 * RING - near(i), RING)
        return (chip,) + role(chip, core)

    def q_copy(i):
        chip, dbl, _, slot = target(i)
        to_core = dbl * core + (1 - dbl) * lax.rem(lax.div(i, 2), 2)
        place = dbl * i + (1 - dbl) * (2 * lax.div(i, 4) + lax.rem(i, 2))
        return pltpu.make_async_remote_copy(
            src_ref=qp_ref.at[slot], dst_ref=q_buf.at[place],
            send_sem=q_send.at[i], recv_sem=q_recv.at[place],
            device_id=(base + chip, tp_base + to_core), device_id_type=MESH,
        )

    q_stays = (owner == core) & ((double == 1) | (core == 0))

    def q_pass(kind):
        def q_start(k, _):
            i = RING - 1 - k
            _, dbl, own, _ = target(i)

            @pl.when((own == core) & (dbl == kind))
            def _():
                q_copy(i).start()

            return 0

        lax.fori_loop(0, RING - 1, q_start, 0)

    def kv_pass(kind):
        def kv_start(i, _):
            _, dbl, own, _ = target(i)

            @pl.when((own == core) & (dbl == kind))
            def _():
                kv_copy(i).start()

            return 0

        lax.fori_loop(1, RING, kv_start, 0)

    q_pass(1)
    @pl.when(q_stays)
    def _():
        pltpu.make_async_copy(qp_ref.at[my_slot], q_buf.at[0], q_recv.at[0]).start()

    @pl.when((owner == core) & jnp.logical_not(q_stays))
    def _():
        q_copy(0).start()

    loads[1].wait()
    loads[2].wait()
    pack_keys(count - z * IMG, k_in, v_in, kg_ref, kvp_ref)

    def kv_copy(i):
        chip, _, _, slot = target(i)
        return pltpu.make_async_remote_copy(
            src_ref=kvp_ref.at[slot], dst_ref=kv_buf.at[i],
            send_sem=kv_send.at[i], recv_sem=kv_recv.at[i],
            device_id=(base + chip, tp), device_id_type=MESH,
        )

    @pl.when(owner == core)
    def _():
        pltpu.make_async_copy(kvp_ref.at[my_slot], kv_buf.at[0], kv_recv.at[0]).start()

    kv_pass(1)
    q_pass(0)
    kv_pass(0)

    loads[4].wait()

    def relay(i):
        return pltpu.make_async_remote_copy(
            src_ref=kv_buf.at[i], dst_ref=kv_buf.at[i],
            send_sem=relay_send.at[i], recv_sem=kv_recv.at[i],
            device_id=sibling, device_id_type=MESH,
        )

    relays = (double == 0) & (owner == core)

    places = 8 + 8 * double
    chunks = 1 + double

    def unpack(s, _):
        pltpu.make_async_copy(q_buf.at[s], q_buf.at[s], q_recv.at[s]).wait()
        packed = q_buf[s].astype(jnp.float32)
        first = lanes((HALF, PAIR)) < HEAD_DIM
        q_all[s, :HALF] = jnp.where(first, packed, 0.0).astype(jnp.bfloat16)
        q_all[s, HALF:] = jnp.where(first, pltpu.roll(packed, HEAD_DIM, 1), 0.0).astype(jnp.bfloat16)
        return 0

    lax.fori_loop(0, places, unpack, 0)
    m_all[...] = jnp.full_like(m_all, -jnp.inf)
    acc_all[...] = jnp.zeros_like(acc_all)

    def arrive(i):
        for n in range(2):
            slot = 2 * i + n
            pltpu.make_async_copy(kv_buf.at[slot], kv_buf.at[slot], kv_recv.at[slot]).wait()

            @pl.when(relays)
            def _():
                relay(slot).start()

        kv = kv_buf[pl.ds(2 * i, 2)].reshape(STEP, PAIR)
        lane = lanes((16, STEP))
        second = lane >= KEYS
        within = jnp.where(second, lane - KEYS, lane)
        rank = jnp.where(second, lax.rem(z + near(2 * i + 1), RING), lax.rem(z + near(2 * i), RING))
        live = (within >= IMG) | (rank * IMG + within < count)
        live = jnp.where(live, 1.0, 0.0).astype(jnp.bfloat16)
        value = jnp.concatenate([kv.T[HEAD_DIM:], live], axis=0)

        return kv, value

    def chunk_step(kv, value, j):
        q = q_all[pl.ds(GROUP * j, GROUP)].reshape(CHUNK, PAIR)
        s = lax.dot_general(kv, q, (((1,), (1,)), ((), ())), preferred_element_type=jnp.float32)
        m_old = m_all[j]
        m_new = jnp.maximum(m_old, jnp.max(s, axis=0, keepdims=True))
        p = jnp.exp2((s - m_new) * LOG2E).astype(jnp.bfloat16)
        decay = jnp.exp2((m_old - m_new) * LOG2E)
        acc_all[j] = acc_all[j] * decay + jnp.dot(value, p, preferred_element_type=jnp.float32)
        m_all[j] = m_new

    def key_step(i, _):
        kv, value = arrive(i)

        def each(j, _):
            chunk_step(kv, value, j)
            return 0

        lax.fori_loop(0, chunks, each, 0)
        return 0

    lax.fori_loop(0, RING // 2 - 1, key_step, 0)

    def home(s):
        i = double * s + (1 - double) * (4 * lax.div(s, 2) + 2 * core + lax.rem(s, 2))
        return lax.rem(z + near(i), RING)

    def o_copy(s, n):
        return pltpu.make_async_remote_copy(
            src_ref=o_stage[n].at[s], dst_ref=o_buf[n].at[my_slot],
            send_sem=o_send.at[s, n], recv_sem=o_recv.at[my_slot, n],
            device_id=(base + home(s), tp_base + owner), device_id_type=MESH,
        )

    def stays(s):
        return (home(s) == z) & (owner == core)

    def o_start(s, n):
        @pl.when(stays(s))
        def _():
            pltpu.make_async_copy(
                o_stage[n].at[s], o_buf[n].at[my_slot], o_recv.at[my_slot, n]
            ).start()

        @pl.when(jnp.logical_not(stays(s)))
        def _():
            o_copy(s, n).start()

    def finish(j):
        out = (acc_all[j, :HEAD_DIM] / acc_all[j, HEAD_DIM : HEAD_DIM + 1]).T
        for b in range(GROUP):
            for n, (first, size) in enumerate(PIECES):
                at = b * IMG + first
                both = [out[at : at + size], out[at + size : at + 2 * size]]
                o_stage[n][GROUP * j + b] = jnp.concatenate(both, axis=1).astype(jnp.bfloat16)
        for b in range(GROUP - 1, -1, -1):
            o_start(GROUP * j + b, 0)

    kv_last, value_last = arrive(RING // 2 - 1)

    def last_chunks(k, _):
        j = chunks - 1 - k
        chunk_step(kv_last, value_last, j)
        finish(j)
        return 0

    lax.fori_loop(0, chunks, last_chunks, 0)

    def o_rest(k, _):
        o_start(places - 1 - k, 1)
        return 0

    lax.fori_loop(0, places, o_rest, 0)
    limit = lax.div(HEADS + 3 - tp, 4)

    def gather(n):
        first, size = PIECES[n]
        for j in range(SLOTS):
            pltpu.make_async_copy(o_buf[n].at[j], o_buf[n].at[j], o_recv.at[j, n]).wait()
            valid = jnp.where(j < limit, 1.0, 0.0)
            got = (o_buf[n][j].astype(jnp.float32) * valid).astype(jnp.bfloat16)
            columns = slice(j * HEAD_DIM, (j + 1) * HEAD_DIM)
            att_ref[first : first + size, columns] = got[:, :HEAD_DIM]
            att_ref[first + size : first + 2 * size, columns] = got[:, HEAD_DIM:]

    def pair_copy(n):
        return pltpu.make_async_remote_copy(
            src_ref=part.at[n, 1 - core], dst_ref=pair_in.at[n],
            send_sem=pair_send.at[n], recv_sem=pair_recv.at[n],
            device_id=sibling, device_id_type=MESH,
        )

    def mate_copy(n):
        return pltpu.make_async_remote_copy(
            src_ref=mate_out.at[n], dst_ref=mate_in.at[n],
            send_sem=mate_send.at[n], recv_sem=mate_recv.at[n],
            device_id=mate, device_id_type=MESH,
        )

    loads[3].wait()
    gates = gate_ref[...].astype(jnp.float32)
    chosen = lax.broadcasted_iota(jnp.int32, gates.shape, 0) == lax.div(pos, RING)
    gate_row = jnp.sum(jnp.where(chosen, gates, 0.0), axis=0, keepdims=True)

    for piece, blocks in ((0, (0, 1)), (1, (2,))):
        gather(piece)
        first, size = PIECES[piece]
        product = jnp.dot(
            att_ref[first : first + 2 * size], w_in[...], preferred_element_type=jnp.float32
        )
        for n in blocks:
            rows = slice(n * ROWS - first, (n + 1) * ROWS - first)
            for t in range(4):
                share = product[rows, t * WIDE : (t + 1) * WIDE]
                part[n, t % 2, t // 2] = share.astype(jnp.bfloat16)
            pair_copy(n).start()
        for n in blocks:
            pair_copy(n).wait_recv()
            both = part[n, core, 1 - side].astype(jnp.float32)
            both += pair_in[n, 1 - side].astype(jnp.float32)
            mate_out[n] = both.astype(jnp.bfloat16)
            mate_copy(n).start()
    for n in range(BLOCKS):
        rows = slice(n * ROWS, (n + 1) * ROWS)
        both = part[n, core, side].astype(jnp.float32) + pair_in[n, side].astype(jnp.float32)
        mate_copy(n).wait_recv()
        projected = both + mate_in[n].astype(jnp.float32)
        updated = res_in[rows].astype(jnp.float32) + gate_row * projected
        out_ref[rows] = updated.astype(jnp.bfloat16)
    for n in range(BLOCKS):
        pair_copy(n).wait_send()
        mate_copy(n).wait_send()

    def drain(i, _):
        @pl.when(target(i)[2] == core)
        def _():
            q_copy(i).wait_send()
            kv_copy(i).wait_send()

        return 0

    lax.fori_loop(1, RING, drain, 0)

    @pl.when((owner == core) & jnp.logical_not(q_stays))
    def _():
        q_copy(0).wait_send()

    @pl.when(relays)
    def _():
        def relay_drain(i, _):
            relay(i).wait_send()
            return 0

        lax.fori_loop(0, RING, relay_drain, 0)

    def o_drain(s, _):
        @pl.when(jnp.logical_not(stays(s)))
        def _():
            o_copy(s, 0).wait_send()
            o_copy(s, 1).wait_send()

        return 0

    lax.fori_loop(0, places, o_drain, 0)


VMEM = pl.BlockSpec(memory_space=pltpu.VMEM)
SMEM = pl.BlockSpec(memory_space=pltpu.SMEM)
HBM = pl.BlockSpec(memory_space=pltpu.HBM)


def local(query, keys, values, q_gain, k_gain, residual, gate, out_weight, image_count):
    bf16, f32 = jnp.bfloat16, jnp.float32
    sem = pltpu.SemaphoreType.DMA
    return pl.pallas_call(
        main_kernel,
        out_shape=jax.ShapeDtypeStruct(residual.shape, bf16),
        in_specs=[SMEM, HBM, HBM, HBM, VMEM, VMEM, HBM, VMEM, HBM],
        out_specs=VMEM,
        scratch_shapes=[
            pltpu.VMEM(query.shape, bf16),
            pltpu.VMEM(keys.shape, bf16),
            pltpu.VMEM(values.shape, bf16),
            pltpu.VMEM(residual.shape, bf16),
            pltpu.VMEM(out_weight.shape, bf16),
            pltpu.VMEM((SLOTS, HALF, PAIR), bf16),
            pltpu.VMEM((SLOTS, KEYS, PAIR), bf16),
            pltpu.VMEM((RING, KEYS, PAIR), bf16),
            pltpu.VMEM((RING, HALF, PAIR), bf16),
            pltpu.VMEM((RING, IMG, PAIR), bf16),
            pltpu.VMEM((2, 1, CHUNK), f32),
            pltpu.VMEM((2, HEAD_DIM + 16, CHUNK), f32),
            pltpu.VMEM((RING, PIECES[0][1], PAIR), bf16),
            pltpu.VMEM((RING, PIECES[1][1], PAIR), bf16),
            pltpu.VMEM((SLOTS, PIECES[0][1], PAIR), bf16),
            pltpu.VMEM((SLOTS, PIECES[1][1], PAIR), bf16),
            pltpu.VMEM((IMG, SLOTS * HEAD_DIM), bf16),
            pltpu.VMEM((BLOCKS, 2, 2, ROWS, WIDE), bf16),
            pltpu.VMEM((BLOCKS, 2, ROWS, WIDE), bf16),
            pltpu.VMEM((BLOCKS, ROWS, WIDE), bf16),
            pltpu.VMEM((BLOCKS, ROWS, WIDE), bf16),
            sem((5,)),
            sem((RING,)), sem((RING,)), sem((RING,)), sem((RING,)),
            sem((RING, 2)), sem((SLOTS, 2)), sem((RING,)),
            sem((BLOCKS,)), sem((BLOCKS,)), sem((BLOCKS,)), sem((BLOCKS,)),
        ],
        compiler_params=pltpu.CompilerParams(
            collective_id=0, has_side_effects=True, vmem_limit_bytes=65_000_000
        ),
        name="attend",
    )(
        image_count, query, keys, values, q_gain.reshape(1, HEAD_DIM), k_gain,
        residual, gate, out_weight,
    )


def solution(mesh):
    placed = (
        P("seq", "tp"),
        P("seq", "tp"),
        P("seq", "tp"),
        P(),
        P(),
        P("seq", "tp"),
        P(None, "tp"),
        P("tp", None),
        P(),
    )
    return jax.shard_map(
        local, mesh=mesh, in_specs=placed, out_specs=P("seq", "tp"), check_vma=False
    )
```

```python
import jax
import jax.numpy as jnp
from jax import lax
from jax.experimental import pallas as pl
from jax.experimental.pallas import tpu as pltpu
from jax.sharding import PartitionSpec as P

HEADS = 38
HEAD_DIM = 64
RING = 16
SLOTS = 10
IMG = 192
KEYS = 224
HALF = IMG // 2
PAIR = 2 * HEAD_DIM
GROUP = 8
CHUNK = GROUP * IMG
STEP = 2 * KEYS
WIDE = 608
BLOCKS = 3
ROWS = IMG // BLOCKS
PIECES = ((0, 64), (128, 32))
LOG2E = 1.4426950408889634
MESH = pl.DeviceIdType.MESH
epsilon = 1e-06


def lanes(shape):
    return lax.broadcasted_iota(jnp.int32, shape, 1)


def pack(low, high):
    first = lanes(low.shape) < HEAD_DIM
    even = jnp.where(first, low, pltpu.roll(high, HEAD_DIM, 1))
    odd = jnp.where(first, pltpu.roll(low, HEAD_DIM, 1), high)
    return even.astype(jnp.bfloat16), odd.astype(jnp.bfloat16)


def normed(value, gain, ones):
    x = value.astype(jnp.float32)
    square = x * x
    high = square.astype(jnp.bfloat16)
    low = (square - high.astype(jnp.float32)).astype(jnp.bfloat16)
    total = jnp.dot(high, ones, preferred_element_type=jnp.float32)
    total += jnp.dot(low, ones, preferred_element_type=jnp.float32)
    inverse = lax.rsqrt(total * (1.0 / HEAD_DIM) + epsilon)
    return (x * inverse * gain).astype(jnp.bfloat16).astype(jnp.float32)


def ones_pair():
    row = lax.broadcasted_iota(jnp.int32, (PAIR, PAIR), 0) < HEAD_DIM
    column = lanes((PAIR, PAIR)) < HEAD_DIM
    return jnp.where(row == column, 1.0, 0.0).astype(jnp.bfloat16)


def pack_queries(q_ref, qg_ref, qp_ref):
    gain = jnp.concatenate([qg_ref[...], qg_ref[...]], axis=1)
    ones = ones_pair()
    for p in range(SLOTS // 2):
        q = normed(q_ref[:, p * PAIR : (p + 1) * PAIR], gain, ones) * HEAD_DIM ** (-0.5)
        qp_ref[2 * p], qp_ref[2 * p + 1] = pack(q[:HALF], q[HALF:])


def pack_keys(left, k_ref, v_ref, kg_ref, kvp_ref):
    gain = jnp.concatenate([kg_ref[...], kg_ref[...]], axis=1)
    ones = ones_pair()
    key_row = lax.broadcasted_iota(jnp.int32, (KEYS, PAIR), 0)
    gain_rows = jnp.where(key_row < IMG, gain[0:1], gain[1:2])
    dead = (key_row < IMG) & (key_row >= left)
    for p in range(SLOTS // 2):
        columns = slice(p * PAIR, (p + 1) * PAIR)
        k = normed(k_ref[:, columns], gain_rows, ones)
        k = jnp.where(dead, k[IMG : IMG + 1], k)
        v = jnp.where(dead, 0.0, v_ref[:, columns].astype(jnp.float32))
        kvp_ref[2 * p], kvp_ref[2 * p + 1] = pack(k, v)


def near(i):
    return RING + (2 * lax.rem(i, 2) - 1) * lax.div(i + 1, 2)


def role(z, core):
    part, quarter = lax.rem(z, 4), lax.div(z, 4)
    double = lax.div(4 - part, 4)
    odd = lax.rem(part, 2)
    middle = (1 - double) * (1 - odd)
    owner = double * core + odd * lax.div(part, 2) + middle * lax.rem(quarter, 2)
    slot = double * quarter + odd * (4 + quarter) + middle * (8 + lax.div(z, 8))
    return double, owner, slot


def main_kernel(
    count_ref, q_hbm, k_hbm, v_hbm, qg_ref, kg_ref, res_hbm, gate_ref, w_hbm, out_ref,
    q_in, k_in, v_in, res_in, w_in, qp_ref, kvp_ref,
    kv_buf, q_buf, q_all, m_all, acc_all,
    o_stage_a, o_stage_b, o_buf_a, o_buf_b, att_ref,
    part, pair_in, mate_out, mate_in, load,
    kv_send, kv_recv, q_send, q_recv, o_send, o_recv, relay_send,
    pair_send, pair_recv, mate_send, mate_recv,
):
    o_stage, o_buf = (o_stage_a, o_stage_b), (o_buf_a, o_buf_b)
    pos = lax.axis_index("seq")
    tp = lax.axis_index("tp")
    z = lax.rem(pos, RING)
    base = pos - z
    core = lax.rem(tp, 2)
    tp_base = tp - core
    double, owner, my_slot = role(z, core)
    side = lax.div(tp, 2)
    mate = (pos, 2 * (1 - side) + core)
    sibling = (pos, tp_base + 1 - core)

    barrier = pltpu.get_barrier_semaphore()
    linear = z * 2 + core

    def greet(i, _):
        peer = lax.rem(linear + i, 2 * RING)
        pl.semaphore_signal(
            barrier,
            inc=1,
            device_id=(base + lax.div(peer, 2), tp_base + lax.rem(peer, 2)),
            device_id_type=MESH,
        )
        return 0

    pltpu.make_async_copy(q_hbm, q_in, load.at[0]).start()
    for low, high in ((8, 25), (1, 8), (25, 32)):
        lax.fori_loop(low, high, greet, 0)
    pl.semaphore_signal(barrier, inc=1, device_id=mate, device_id_type=MESH)
    loads = [
        pltpu.make_async_copy(source, place, load.at[n])
        for n, (source, place) in enumerate(
            [(q_hbm, q_in), (k_hbm, k_in), (v_hbm, v_in), (res_hbm, res_in), (w_hbm, w_in)]
        )
    ]
    for copy in loads[1:]:
        copy.start()

    count = count_ref[lax.div(pos, RING)]
    loads[0].wait()
    pack_queries(q_in, qg_ref, qp_ref)
    pl.semaphore_wait(barrier, 2 * RING)

    def target(i):
        chip = lax.rem(z + 2 * RING - near(i), RING)
        return (chip,) + role(chip, core)

    def q_copy(i):
        chip, dbl, _, slot = target(i)
        to_core = dbl * core + (1 - dbl) * lax.rem(lax.div(i, 2), 2)
        place = dbl * i + (1 - dbl) * (2 * lax.div(i, 4) + lax.rem(i, 2))
        return pltpu.make_async_remote_copy(
            src_ref=qp_ref.at[slot], dst_ref=q_buf.at[place],
            send_sem=q_send.at[i], recv_sem=q_recv.at[place],
            device_id=(base + chip, tp_base + to_core), device_id_type=MESH,
        )

    q_stays = (owner == core) & ((double == 1) | (core == 0))

    def q_pass(kind):
        def q_start(k, _):
            i = RING - 1 - k
            _, dbl, own, _ = target(i)

            @pl.when((own == core) & (dbl == kind))
            def _():
                q_copy(i).start()

            return 0

        lax.fori_loop(0, RING - 1, q_start, 0)

    def kv_pass(kind):
        def kv_start(i, _):
            _, dbl, own, _ = target(i)

            @pl.when((own == core) & (dbl == kind))
            def _():
                kv_copy(i).start()

            return 0

        lax.fori_loop(1, RING, kv_start, 0)

    q_pass(1)
    @pl.when(q_stays)
    def _():
        pltpu.make_async_copy(qp_ref.at[my_slot], q_buf.at[0], q_recv.at[0]).start()

    @pl.when((owner == core) & jnp.logical_not(q_stays))
    def _():
        q_copy(0).start()

    loads[1].wait()
    loads[2].wait()
    pack_keys(count - z * IMG, k_in, v_in, kg_ref, kvp_ref)

    def kv_copy(i):
        chip, _, _, slot = target(i)
        return pltpu.make_async_remote_copy(
            src_ref=kvp_ref.at[slot], dst_ref=kv_buf.at[i],
            send_sem=kv_send.at[i], recv_sem=kv_recv.at[i],
            device_id=(base + chip, tp), device_id_type=MESH,
        )

    @pl.when(owner == core)
    def _():
        pltpu.make_async_copy(kvp_ref.at[my_slot], kv_buf.at[0], kv_recv.at[0]).start()

    kv_pass(1)
    q_pass(0)
    kv_pass(0)

    loads[4].wait()

    def relay(i):
        return pltpu.make_async_remote_copy(
            src_ref=kv_buf.at[i], dst_ref=kv_buf.at[i],
            send_sem=relay_send.at[i], recv_sem=kv_recv.at[i],
            device_id=sibling, device_id_type=MESH,
        )

    relays = (double == 0) & (owner == core)

    places = 8 + 8 * double
    chunks = 1 + double

    def unpack(s, _):
        pltpu.make_async_copy(q_buf.at[s], q_buf.at[s], q_recv.at[s]).wait()
        packed = q_buf[s].astype(jnp.float32)
        first = lanes((HALF, PAIR)) < HEAD_DIM
        q_all[s, :HALF] = jnp.where(first, packed, 0.0).astype(jnp.bfloat16)
        q_all[s, HALF:] = jnp.where(first, pltpu.roll(packed, HEAD_DIM, 1), 0.0).astype(jnp.bfloat16)
        return 0

    m_all[...] = jnp.full_like(m_all, -jnp.inf)
    acc_all[...] = jnp.zeros_like(acc_all)
    lax.fori_loop(0, places, unpack, 0)

    def arrive(i):
        for n in range(2):
            slot = 2 * i + n
            pltpu.make_async_copy(kv_buf.at[slot], kv_buf.at[slot], kv_recv.at[slot]).wait()

            @pl.when(relays)
            def _():
                relay(slot).start()

        kv = kv_buf[pl.ds(2 * i, 2)].reshape(STEP, PAIR)
        lane = lanes((16, STEP))
        second = lane >= KEYS
        within = jnp.where(second, lane - KEYS, lane)
        rank = jnp.where(second, lax.rem(z + near(2 * i + 1), RING), lax.rem(z + near(2 * i), RING))
        live = (within >= IMG) | (rank * IMG + within < count)
        live = jnp.where(live, 1.0, 0.0).astype(jnp.bfloat16)
        value = jnp.concatenate([kv.T[HEAD_DIM:], live], axis=0)

        return kv, value

    def chunk_step(kv, value, j):
        q = q_all[pl.ds(GROUP * j, GROUP)].reshape(CHUNK, PAIR)
        s = lax.dot_general(kv, q, (((1,), (1,)), ((), ())), preferred_element_type=jnp.float32)
        m_old = m_all[j]
        m_new = jnp.maximum(m_old, jnp.max(s, axis=0, keepdims=True))
        p = jnp.exp2((s - m_new) * LOG2E).astype(jnp.bfloat16)
        decay = jnp.exp2((m_old - m_new) * LOG2E)
        acc_all[j] = acc_all[j] * decay + jnp.dot(value, p, preferred_element_type=jnp.float32)
        m_all[j] = m_new

    def key_step(i, _):
        kv, value = arrive(i)

        def each(j, _):
            chunk_step(kv, value, j)
            return 0

        lax.fori_loop(0, chunks, each, 0)
        return 0

    lax.fori_loop(0, RING // 2 - 1, key_step, 0)

    def home(s):
        i = double * s + (1 - double) * (4 * lax.div(s, 2) + 2 * core + lax.rem(s, 2))
        return lax.rem(z + near(i), RING)

    def o_copy(s, n):
        return pltpu.make_async_remote_copy(
            src_ref=o_stage[n].at[s], dst_ref=o_buf[n].at[my_slot],
            send_sem=o_send.at[s, n], recv_sem=o_recv.at[my_slot, n],
            device_id=(base + home(s), tp_base + owner), device_id_type=MESH,
        )

    def stays(s):
        return (home(s) == z) & (owner == core)

    def o_start(s, n):
        @pl.when(stays(s))
        def _():
            pltpu.make_async_copy(
                o_stage[n].at[s], o_buf[n].at[my_slot], o_recv.at[my_slot, n]
            ).start()

        @pl.when(jnp.logical_not(stays(s)))
        def _():
            o_copy(s, n).start()

    def finish(j):
        out = (acc_all[j, :HEAD_DIM] / acc_all[j, HEAD_DIM : HEAD_DIM + 1]).T
        for b in range(GROUP):
            for n, (first, size) in enumerate(PIECES):
                at = b * IMG + first
                both = [out[at : at + size], out[at + size : at + 2 * size]]
                o_stage[n][GROUP * j + b] = jnp.concatenate(both, axis=1).astype(jnp.bfloat16)
        for b in range(GROUP - 1, -1, -1):
            o_start(GROUP * j + b, 0)

    kv_last, value_last = arrive(RING // 2 - 1)

    def last_chunks(k, _):
        j = chunks - 1 - k
        chunk_step(kv_last, value_last, j)
        finish(j)
        return 0

    lax.fori_loop(0, chunks, last_chunks, 0)

    def o_rest(k, _):
        o_start(places - 1 - k, 1)
        return 0

    lax.fori_loop(0, places, o_rest, 0)
    limit = lax.div(HEADS + 3 - tp, 4)

    def gather(n):
        first, size = PIECES[n]
        for j in range(SLOTS):
            pltpu.make_async_copy(o_buf[n].at[j], o_buf[n].at[j], o_recv.at[j, n]).wait()
            valid = jnp.where(j < limit, 1.0, 0.0)
            got = (o_buf[n][j].astype(jnp.float32) * valid).astype(jnp.bfloat16)
            columns = slice(j * HEAD_DIM, (j + 1) * HEAD_DIM)
            att_ref[first : first + size, columns] = got[:, :HEAD_DIM]
            att_ref[first + size : first + 2 * size, columns] = got[:, HEAD_DIM:]

    def pair_copy(n):
        return pltpu.make_async_remote_copy(
            src_ref=part.at[n, 1 - core], dst_ref=pair_in.at[n],
            send_sem=pair_send.at[n], recv_sem=pair_recv.at[n],
            device_id=sibling, device_id_type=MESH,
        )

    def mate_copy(n):
        return pltpu.make_async_remote_copy(
            src_ref=mate_out.at[n], dst_ref=mate_in.at[n],
            send_sem=mate_send.at[n], recv_sem=mate_recv.at[n],
            device_id=mate, device_id_type=MESH,
        )

    loads[3].wait()
    gates = gate_ref[...].astype(jnp.float32)
    chosen = lax.broadcasted_iota(jnp.int32, gates.shape, 0) == lax.div(pos, RING)
    gate_row = jnp.sum(jnp.where(chosen, gates, 0.0), axis=0, keepdims=True)

    for piece, blocks in ((0, (0, 1)), (1, (2,))):
        gather(piece)
        first, size = PIECES[piece]
        product = jnp.dot(
            att_ref[first : first + 2 * size], w_in[...], preferred_element_type=jnp.float32
        )
        for n in blocks:
            rows = slice(n * ROWS - first, (n + 1) * ROWS - first)
            for t in range(4):
                share = product[rows, t * WIDE : (t + 1) * WIDE]
                part[n, t % 2, t // 2] = share.astype(jnp.bfloat16)
            pair_copy(n).start()
        for n in blocks:
            pair_copy(n).wait_recv()
            both = part[n, core, 1 - side].astype(jnp.float32)
            both += pair_in[n, 1 - side].astype(jnp.float32)
            mate_out[n] = both.astype(jnp.bfloat16)
            mate_copy(n).start()
    for n in range(BLOCKS):
        rows = slice(n * ROWS, (n + 1) * ROWS)
        both = part[n, core, side].astype(jnp.float32) + pair_in[n, side].astype(jnp.float32)
        mate_copy(n).wait_recv()
        projected = both + mate_in[n].astype(jnp.float32)
        updated = res_in[rows].astype(jnp.float32) + gate_row * projected
        out_ref[rows] = updated.astype(jnp.bfloat16)
    for n in range(BLOCKS):
        pair_copy(n).wait_send()
        mate_copy(n).wait_send()

    def drain(i, _):
        @pl.when(target(i)[2] == core)
        def _():
            q_copy(i).wait_send()
            kv_copy(i).wait_send()

        return 0

    lax.fori_loop(1, RING, drain, 0)

    @pl.when((owner == core) & jnp.logical_not(q_stays))
    def _():
        q_copy(0).wait_send()

    @pl.when(relays)
    def _():
        def relay_drain(i, _):
            relay(i).wait_send()
            return 0

        lax.fori_loop(0, RING, relay_drain, 0)

    def o_drain(s, _):
        @pl.when(jnp.logical_not(stays(s)))
        def _():
            o_copy(s, 0).wait_send()
            o_copy(s, 1).wait_send()

        return 0

    lax.fori_loop(0, places, o_drain, 0)


VMEM = pl.BlockSpec(memory_space=pltpu.VMEM)
SMEM = pl.BlockSpec(memory_space=pltpu.SMEM)
HBM = pl.BlockSpec(memory_space=pltpu.HBM)


def local(query, keys, values, q_gain, k_gain, residual, gate, out_weight, image_count):
    bf16, f32 = jnp.bfloat16, jnp.float32
    sem = pltpu.SemaphoreType.DMA
    return pl.pallas_call(
        main_kernel,
        out_shape=jax.ShapeDtypeStruct(residual.shape, bf16),
        in_specs=[SMEM, HBM, HBM, HBM, VMEM, VMEM, HBM, VMEM, HBM],
        out_specs=VMEM,
        scratch_shapes=[
            pltpu.VMEM(query.shape, bf16),
            pltpu.VMEM(keys.shape, bf16),
            pltpu.VMEM(values.shape, bf16),
            pltpu.VMEM(residual.shape, bf16),
            pltpu.VMEM(out_weight.shape, bf16),
            pltpu.VMEM((SLOTS, HALF, PAIR), bf16),
            pltpu.VMEM((SLOTS, KEYS, PAIR), bf16),
            pltpu.VMEM((RING, KEYS, PAIR), bf16),
            pltpu.VMEM((RING, HALF, PAIR), bf16),
            pltpu.VMEM((RING, IMG, PAIR), bf16),
            pltpu.VMEM((2, 1, CHUNK), f32),
            pltpu.VMEM((2, HEAD_DIM + 16, CHUNK), f32),
            pltpu.VMEM((RING, PIECES[0][1], PAIR), bf16),
            pltpu.VMEM((RING, PIECES[1][1], PAIR), bf16),
            pltpu.VMEM((SLOTS, PIECES[0][1], PAIR), bf16),
            pltpu.VMEM((SLOTS, PIECES[1][1], PAIR), bf16),
            pltpu.VMEM((IMG, SLOTS * HEAD_DIM), bf16),
            pltpu.VMEM((BLOCKS, 2, 2, ROWS, WIDE), bf16),
            pltpu.VMEM((BLOCKS, 2, ROWS, WIDE), bf16),
            pltpu.VMEM((BLOCKS, ROWS, WIDE), bf16),
            pltpu.VMEM((BLOCKS, ROWS, WIDE), bf16),
            sem((5,)),
            sem((RING,)), sem((RING,)), sem((RING,)), sem((RING,)),
            sem((RING, 2)), sem((SLOTS, 2)), sem((RING,)),
            sem((BLOCKS,)), sem((BLOCKS,)), sem((BLOCKS,)), sem((BLOCKS,)),
        ],
        compiler_params=pltpu.CompilerParams(
            collective_id=0, has_side_effects=True, vmem_limit_bytes=65_000_000
        ),
        name="attend",
    )(
        image_count, query, keys, values, q_gain.reshape(1, HEAD_DIM), k_gain,
        residual, gate, out_weight,
    )


def solution(mesh):
    placed = (
        P("seq", "tp"),
        P("seq", "tp"),
        P("seq", "tp"),
        P(),
        P(),
        P("seq", "tp"),
        P(None, "tp"),
        P("tp", None),
        P(),
    )
    return jax.shard_map(
        local, mesh=mesh, in_specs=placed, out_specs=P("seq", "tp"), check_vma=False
    )
```
